512 devices in a mesh: mem: 64 (over z, x, core), bal: 8 (over y).
Axes of the slice: x: 4, y: 8, z: 8, core: 2. Of those that a mesh axis runs over, the one named last changes fastest.
Arguments:
- background_trials: bfloat16 [256, 1024, 256], P('mem', 'bal'), may hold values from -6 to 6
- mapped_readings: bfloat16 [256, 1024, 2048], P('mem', 'bal'), may hold values from -6 to 6
- measured_data: float32 [1024, 2048], P('bal'), may hold values from -9 to 9
- inverse_error_variance: float32 [1024, 2048], P('bal'), may hold values from 0.05 to 1
- measured_row_tally: int32 [1024], P('bal'), may hold values from 16 to 2032, as said below
Outputs:
- analysis: bfloat16 [256, 1024, 256], P('mem', 'bal')
The draws below stay inside these ranges and needn't reach their ends.
Inputs may be any that keep to these rules, and one draw needn't show every extreme that they name: measured_row_tally[p] live rows, the first ones of patch p's block; in each aligned group of 2 consecutive patches the counts sum to at most 2048, and some group sums to exactly 2048.
All inputs are finite; a program needn't handle non-finite values.
Results may differ from the reference program's by a relative error of at most 0.0057.
Values may be sent and summed in bfloat16 or wider, within the bound.
No kernel may reach another device: no remote copies, remote signals or barrier semaphores. Data moves between devices by JAX's collectives and lax.ppermute only.
A program may use at most 64 MiB of HBM per device.

```python
import math
import jax
import jax.numpy as jnp
from jax import lax

MODEL_TRIALS = 256
TILE_DIMENSION = 256
MAX_OBS_SLOTS = 2048
PAT_DEV = 2
NS_ITERS = 7
TILE_AMOUNT = 1024


def draw_measured_row_tally(key, part):
    groups = TILE_AMOUNT // PAT_DEV
    first = jax.random.fold_in(key, 11)
    second = jax.random.fold_in(key, 12)
    third = jax.random.fold_in(key, 13)
    fourth = jax.random.fold_in(key, 14)
    fifth = jax.random.fold_in(key, 15)
    level = jax.random.randint(first, (groups,), 0, 3)
    cut = jax.random.randint(second, (groups,), 0, MAX_OBS_SLOTS // 16 + 1)
    top = jnp.right_shift(jnp.full((groups,), MAX_OBS_SLOTS, jnp.int32), level)
    total = jnp.maximum(top - cut, 16 * PAT_DEV)
    weights = jax.random.randint(third, (groups, PAT_DEV), 1, 9)
    spare = total - 16 * PAT_DEV
    share = 16 + spare[:, None] * weights // jnp.sum(weights, axis=1, keepdims=True)
    before = jnp.sum(share[:, :PAT_DEV - 1], axis=1)
    counts = jnp.concatenate([share[:, :PAT_DEV - 1], (total - before)[:, None]], axis=1)
    spot_full = jax.random.randint(fourth, (), 0, groups)
    spot_low = (spot_full + 1 + jax.random.randint(fifth, (), 0, groups - 1)) % groups
    slots = lax.iota(jnp.int32, PAT_DEV)
    full_row = jnp.where(slots == PAT_DEV - 1, MAX_OBS_SLOTS - 16 * (PAT_DEV - 1), 16)
    low_row = jnp.full((PAT_DEV,), 16, jnp.int32)
    rows = lax.iota(jnp.int32, groups)[:, None]
    counts = jnp.where(rows == spot_full, full_row[None, :], counts)
    counts = jnp.where(rows == spot_low, low_row[None, :], counts)
    return counts.reshape(TILE_AMOUNT).astype(jnp.int32)


def levels(own_key, dims, cuts, low, high):
    loudness, own = 1.0, jax.random.fold_in(own_key, 6)
    for position, parts in cuts:
        draws = jnp.exp(jax.random.uniform(jax.random.fold_in(own, position), (parts,), jnp.float32, low / len(cuts), high / len(cuts)))
        loudness = loudness * jnp.repeat(draws, dims[position] // parts).reshape([-1 if axis == position else 1 for axis in range(len(dims))])
    return loudness


def scatter_about(own_key, dims, scale, limit, pieces=(), held_as=jnp.bfloat16):
    gain = levels(own_key, dims, pieces, -0.22, 0.18) if pieces else 1.0
    array = jax.random.normal(own_key, dims, jnp.float32) * scale * gain
    return jnp.minimum(jnp.maximum(array, -limit), limit).astype(held_as)


def setup_inputs(seed: int = 0) -> dict:
    arg_keys = jax.random.split(jax.random.key(seed), 6)
    return {
        "background_trials": scatter_about(arg_keys[0], (MODEL_TRIALS, TILE_AMOUNT, TILE_DIMENSION), 1.0, 6.0, ((0, 64), (1, 8))),
        "mapped_readings": scatter_about(arg_keys[1], (MODEL_TRIALS, TILE_AMOUNT, MAX_OBS_SLOTS), 1.0, 6.0, ((0, 64), (1, 8))),
        "measured_data": scatter_about(arg_keys[2], (TILE_AMOUNT, MAX_OBS_SLOTS), 1.5, 9.0, ((0, 8),), jnp.float32),
        "inverse_error_variance": jnp.clip(jnp.exp(math.log(1.0) - 2.9957323 * jax.random.uniform(arg_keys[3], (TILE_AMOUNT, MAX_OBS_SLOTS), jnp.float32) ** levels(arg_keys[3], (TILE_AMOUNT, MAX_OBS_SLOTS), ((0, 8),), -0.2, 0.2)), 0.05, 1.0),
        "measured_row_tally": draw_measured_row_tally(jax.random.fold_in(arg_keys[5], 71), 0),
    }


def prepare(ens, value, prec, count):
    rows = lax.iota(jnp.int32, ens.shape[1])
    mask = (rows < count).astype(jnp.float32)
    weight = mask * jnp.sqrt(prec)
    obs_mean = lax.optimization_barrier(jnp.mean(ens, axis=0, dtype=jnp.float32))
    scaled = ((ens.astype(jnp.float32) - obs_mean) * weight).astype(jnp.bfloat16)
    misfit = weight * (value - obs_mean)
    vector = jnp.dot(scaled.astype(jnp.float32), misfit, precision=lax.Precision.HIGHEST)
    return (scaled, vector)

def complete_step(gram, vector, region_variables):
    members = gram.shape[0]
    identity = jnp.eye(members, dtype=jnp.float32)
    amat = gram + (members - 1.0) * identity
    frobenius = jnp.sqrt(jnp.sum(amat * amat))
    iterate = amat / frobenius
    inverse = identity
    for step in range(NS_ITERS):
        middle = 1.5 * identity - 0.5 * jnp.dot(inverse, iterate, precision=lax.Precision.HIGHEST)
        iterate = jnp.dot(iterate, middle, precision=lax.Precision.HIGHEST)
        inverse = jnp.dot(middle, inverse, precision=lax.Precision.HIGHEST)
    spread = jnp.sqrt((members - 1.0) / frobenius) * inverse
    inner = jnp.dot(inverse, vector, precision=lax.Precision.HIGHEST)
    mean_weights = jnp.dot(inverse, inner, precision=lax.Precision.HIGHEST) / frobenius
    transform = (spread + mean_weights[:, None]).astype(jnp.bfloat16)
    state_mean = lax.optimization_barrier(jnp.mean(region_variables, axis=0, dtype=jnp.float32))
    perturb = (region_variables.astype(jnp.float32) - state_mean).astype(jnp.bfloat16)
    moved = jnp.dot(transform.T, perturb, preferred_element_type=jnp.float32)
    return (state_mean + moved).astype(jnp.bfloat16)

def reference(background_trials, mapped_readings, measured_data, inverse_error_variance, measured_row_tally):

    def solitary_tile(region_number):
        region_variables = lax.dynamic_index_in_dim(background_trials, region_number, 1, keepdims=False)
        ens = lax.dynamic_index_in_dim(mapped_readings, region_number, 1, keepdims=False)
        scaled, vector = prepare(ens, measured_data[region_number], inverse_error_variance[region_number], measured_row_tally[region_number])
        gram = jnp.dot(scaled, scaled.T, preferred_element_type=jnp.float32)
        return complete_step(gram, vector, region_variables)
    corrected_trials = lax.map(solitary_tile, jnp.arange(background_trials.shape[1], dtype=jnp.int32))
    return jnp.transpose(corrected_trials, (1, 0, 2))
```

```python
import functools

import jax
import jax.numpy as jnp
from jax import lax
from jax.experimental import pallas as pl
from jax.experimental.pallas import tpu as pltpu
from jax.sharding import PartitionSpec as P

NS_ITERS = 7
F32 = jnp.float32
BF16 = jnp.bfloat16
PACK_VMEM = 56 * 1024 * 1024
ANALYSE_VMEM = 20 * 1024 * 1024


def iotas(rows, columns):
    return (
        lax.broadcasted_iota(jnp.int32, (rows, columns), 0),
        lax.broadcasted_iota(jnp.int32, (rows, columns), 1),
    )


def one_hot(test):
    return jnp.where(test, 1.0, 0.0).astype(BF16)


def mm(a, b):
    return jnp.dot(a, b, preferred_element_type=F32)


def mm_nt(a, b):
    return lax.dot_general(a, b, (((1,), (1,)), ((), ())), preferred_element_type=F32)


def flip(size):
    r, c = iotas(size, size)
    return one_hot(r + c == size - 1)


def pack_kernel(tally_ref, ens_ref, state_ref, packed_ref):
    pairs = packed_ref.shape[0] // 8
    patches = 2 * pairs
    half = ens_ref.shape[2] // 2
    block = pl.program_id(0)
    rows = 8 * pairs
    r, k = iotas(rows, 2 * rows)
    pair, top, member = r >> 3, (r >> 2) & 1, r & 3
    take_a = one_hot(k == top * rows + member * patches + 2 * pair)
    take_b = one_hot(k == (1 - top) * rows + member * patches + 2 * pair + 1)
    x = jnp.concatenate(
        [
            ens_ref[:, :, :half].reshape(rows, half),
            ens_ref[:, :, half:].reshape(rows, half),
        ],
        axis=0,
    )
    first = mm(take_a, x)
    second = mm(take_b, x).astype(BF16)
    r1, l1 = iotas(rows, tally_ref.shape[1])
    wanted = l1 == 2 * (block * pairs + (r1 >> 3))
    limit = jnp.sum(jnp.where(wanted, tally_ref[...].astype(F32), 0.0), axis=1, keepdims=True)
    limit = limit - jnp.where((r1[:, :1] >> 2) & 1 == 1, float(half), 0.0)
    turn = flip(256)
    parts = half // 256
    for q in range(parts):
        lanes = slice(q * 256, (q + 1) * 256)
        back = slice((parts - 1 - q) * 256, (parts - q) * 256)
        _, slot = iotas(rows, 256)
        slot = (slot + q * 256).astype(F32)
        packed_ref[:, lanes] = jnp.where(
            slot < limit, first[:, lanes], mm(second[:, back], turn)
        ).astype(BF16)
    r2, k2 = iotas(rows, rows)
    take_s = one_hot(k2 == (r2 & 3) * patches + (r2 >> 2))
    packed_ref[:, half:] = mm(take_s, state_ref[...].reshape(rows, state_ref.shape[2])).astype(BF16)


def pack(tally, ens, state, interpret=False):
    members, patches, slots = ens.shape
    width = state.shape[2]
    steps = 2
    per = patches // steps
    rows = 4 * patches
    return pl.pallas_call(
        pack_kernel,
        grid=(steps,),
        in_specs=[
            pl.BlockSpec((1, patches), lambda i: (0, 0)),
            pl.BlockSpec((members, per, slots), lambda i: (0, i, 0)),
            pl.BlockSpec((members, per, width), lambda i: (0, i, 0)),
        ],
        out_specs=pl.BlockSpec((rows // steps, slots // 2 + width), lambda i: (i, 0)),
        out_shape=jax.ShapeDtypeStruct((rows, slots // 2 + width), BF16),
        compiler_params=pltpu.CompilerParams(vmem_limit_bytes=PACK_VMEM),
        cost_estimate=pl.CostEstimate(
            flops=10**9, bytes_accessed=5 * 2**20, transcendentals=0
        ),
        interpret=interpret,
    )(tally.reshape(1, patches), ens, state)


def weights_kernel(me_ref, tally_ref, value_ref, prec_ref, out_ref):
    slots = value_ref.shape[1]
    row = 2 * (me_ref[0] % 4)
    count_a = tally_ref[2 * me_ref[0]]
    count_b = tally_ref[2 * me_ref[0] + 1]
    parts = slots // 256
    value = value_ref[...]
    prec = prec_ref[...]
    which, slot = iotas(8, slots)

    def pick(x, i):
        return jnp.sum(jnp.where(which == row + i, x, 0.0), axis=0, keepdims=True)

    value_b = pick(value, 1)
    prec_b = pick(prec, 1)
    cut = [b[:, i * 256 : (i + 1) * 256] for b in (value_b, prec_b) for i in range(parts)]
    r, c = iotas(256, 256)
    turn = jnp.where(r + c == 255, 1.0, 0.0)
    turned = jnp.dot(
        jnp.concatenate(cut, axis=0),
        turn,
        precision=lax.Precision.HIGHEST,
        preferred_element_type=F32,
    )
    back = [
        jnp.concatenate(
            [turned[j * parts + i : j * parts + i + 1] for i in reversed(range(parts))], axis=1
        )
        for j in range(2)
    ]
    slot = slot[:1]
    is_a = slot < count_a
    is_b = slot >= slots - count_b
    weight_a = jnp.where(is_a, jnp.sqrt(pick(prec, 0)), 0.0)
    weight_b = jnp.where(is_b & ~is_a, jnp.sqrt(back[1]), 0.0)
    seen = jnp.where(is_a, pick(value, 0), back[0])
    out_ref[0:1, :] = weight_a
    out_ref[1:2, :] = weight_b
    out_ref[2:3, :] = seen
    out_ref[3:8, :] = jnp.zeros((5, slots), F32)


def pair_weights(me, tally, value, prec, interpret=False):
    slots = value.shape[1]
    return pl.pallas_call(
        weights_kernel,
        grid_spec=pltpu.PrefetchScalarGridSpec(
            num_scalar_prefetch=2,
            grid=(1,),
            in_specs=[pl.BlockSpec((8, slots), lambda i, me, t: (me[0] // 4, 0))] * 2,
            out_specs=pl.BlockSpec((8, slots), lambda i, me, t: (0, 0)),
        ),
        out_shape=jax.ShapeDtypeStruct((8, slots), F32),
        compiler_params=pltpu.CompilerParams(vmem_limit_bytes=16 * 1024 * 1024),
        interpret=interpret,
    )(me, tally, value, prec)


def split(x):
    hi = x.astype(BF16)
    return hi, (x - hi.astype(F32)).astype(BF16)


def mm3(a, b):
    ah, al = a
    bh, bl = b
    return mm(
        jnp.concatenate([ah, ah, al], axis=1), jnp.concatenate([bh, bl, bh], axis=0)
    )


def newton_schulz(ts, eye):
    zs = [1.5 * eye - 0.5 * t for t in ts]
    for step in range(1, NS_ITERS):
        cut = [split(t) for t in ts]
        squares = [mm3(c, c) for c in cut]
        cubes = [mm3(c, split(q)) for c, q in zip(cut, squares)]
        ts = [2.25 * t - 1.5 * q + 0.25 * u for t, q, u in zip(ts, squares, cubes)]
        if step < 4:
            zs = [1.5 * z - 0.5 * mm3(split(t), split(z)) for t, z in zip(ts, zs)]
        else:
            zs = [z + 0.5 * mm3(split(eye - t), split(z)) for t, z in zip(ts, zs)]
    return zs


def centring_matrix(part):
    r, k = iotas(264, 512)
    ours = (k >> 2) & 1 == part
    own = k == (r >> 2) * 8 + part * 4 + (r & 3)
    share = jnp.where(r < 256, -1.0 / 256.0, 1.0 / 256.0)
    return (jnp.where(ours, share, 0.0) + jnp.where(own & (r < 256), 1.0, 0.0)).astype(BF16)


def analysis_kernel(recv_ref, rows_ref, out_ref, s_ref, all_ref, perturb_ref):
    slots = rows_ref.shape[1]
    half = slots // 2
    means, middles = [], []
    for part in range(2):
        centre = centring_matrix(part)
        for q in range(half // 256):
            at = slice(part * half + q * 256, part * half + (q + 1) * 256)
            apart = mm(centre, recv_ref[:, q * 256 : (q + 1) * 256])
            means.append(apart[256:257])
            apart = apart[:256]
            weight_a, weight_b = rows_ref[0:1, at], rows_ref[1:2, at]
            s_ref[0:256, at] = (apart * weight_a).astype(BF16)
            s_ref[256:512, at] = (apart * weight_b).astype(BF16)
            all_ref[:, at] = (apart * (weight_a + weight_b)).astype(BF16)
        apart = mm(centre, recv_ref[:, half:])
        middles.append(apart[256:257])
        perturb_ref[part] = apart[:256].astype(BF16)
    mean = jnp.concatenate(means, axis=1)
    weight_a, weight_b, seen = rows_ref[0:1, :], rows_ref[1:2, :], rows_ref[2:3, :]
    rest = []
    for w in (weight_a, weight_b):
        left = w * (seen - mean)
        for _ in range(3):
            top = left.astype(BF16).astype(F32)
            rest.append(top)
            left = left - top
    rest += [jnp.zeros_like(mean)] * 10
    s_ref[512:528, :] = jnp.concatenate(rest, axis=0).astype(BF16)
    both = mm_nt(s_ref[...], all_ref[...])
    r, c = iotas(256, 256)
    eye = jnp.where(r == c, 1.0, 0.0)
    amat = [both[256 * p : 256 * (p + 1)] + 255.0 * eye for p in range(2)]
    fro = [jnp.sqrt(jnp.sum(a * a)) for a in amat]
    z = newton_schulz([a * (1.0 / f) for a, f in zip(amat, fro)], eye)
    done = []
    for p in range(2):
        v = jnp.sum(both[512 + 3 * p : 515 + 3 * p], axis=0, keepdims=True)
        inner = jnp.sum(z[p] * v, axis=1, keepdims=True)
        mean_weights = jnp.sum(z[p] * inner, axis=0, keepdims=True) / fro[p]
        transform = (jnp.sqrt(255.0 / fro[p]) * z[p] + mean_weights).astype(BF16)
        done.append((middles[p] + mm(transform, perturb_ref[p])).astype(BF16))
    k, r = iotas(256, 256)
    scatter = one_hot(k == ((r & 127) >> 2) * 8 + (r >> 7) * 4 + (r & 3))
    for g in range(2):
        pair = jnp.concatenate([d[128 * g : 128 * (g + 1)] for d in done], axis=0)
        out_ref[256 * g : 256 * (g + 1), :] = mm(scatter, pair).astype(BF16)


def analyse(recv, rows, interpret=False):
    total, wide = recv.shape
    slots = rows.shape[1]
    width = wide - slots // 2
    return pl.pallas_call(
        analysis_kernel,
        out_shape=jax.ShapeDtypeStruct((total, width), BF16),
        scratch_shapes=[
            pltpu.VMEM((528, slots), BF16),
            pltpu.VMEM((256, slots), BF16),
            pltpu.VMEM((2, 256, width), BF16),
        ],
        compiler_params=pltpu.CompilerParams(vmem_limit_bytes=ANALYSE_VMEM),
        cost_estimate=pl.CostEstimate(
            flops=5 * 10**9, bytes_accessed=2 * 2**20, transcendentals=0
        ),
        interpret=interpret,
    )(recv, rows)


def unpack_kernel(recv_ref, out_ref):
    r, k = iotas(256, 256)
    gather = one_hot(k == (r & 63) * 4 + (r >> 6))
    for g in range(2):
        moved = mm(gather, recv_ref[256 * g : 256 * (g + 1), :]).astype(BF16)
        out_ref[:, 64 * g : 64 * (g + 1), :] = moved.reshape(4, 64, recv_ref.shape[1])


def unpack(recv, interpret=False):
    rows, width = recv.shape
    return pl.pallas_call(
        unpack_kernel,
        out_shape=jax.ShapeDtypeStruct((4, rows // 4, width), BF16),
        compiler_params=pltpu.CompilerParams(vmem_limit_bytes=16 * 1024 * 1024),
        interpret=interpret,
    )(recv)


def exchange(x):
    return lax.all_to_all(x, "mem", split_axis=0, concat_axis=0, tiled=True)


def on_device(
    background_trials, mapped_readings, measured_data, inverse_error_variance, measured_row_tally
):
    me = lax.axis_index("mem").astype(jnp.int32).reshape(1)
    packed = pack(measured_row_tally, mapped_readings, background_trials)
    received = exchange(packed)
    rows = pair_weights(me, measured_row_tally, measured_data, inverse_error_variance)
    return unpack(exchange(analyse(received, rows)))


def solution(mesh):
    return jax.shard_map(
        on_device,
        mesh=mesh,
        in_specs=(
            P("mem", "bal", None),
            P("mem", "bal", None),
            P("bal", None),
            P("bal", None),
            P("bal"),
        ),
        out_specs=P("mem", "bal", None),
        check_vma=False,
    )
```

```python
import functools

import jax
import jax.numpy as jnp
from jax import lax
from jax.experimental import pallas as pl
from jax.experimental.pallas import tpu as pltpu
from jax.sharding import PartitionSpec as P

NS_ITERS = 7
F32 = jnp.float32
BF16 = jnp.bfloat16
PACK_VMEM = 56 * 1024 * 1024
ANALYSE_VMEM = 20 * 1024 * 1024


def iotas(rows, columns):
    return (
        lax.broadcasted_iota(jnp.int32, (rows, columns), 0),
        lax.broadcasted_iota(jnp.int32, (rows, columns), 1),
    )


def one_hot(test):
    return jnp.where(test, 1.0, 0.0).astype(BF16)


def mm(a, b):
    return jnp.dot(a, b, preferred_element_type=F32)


def mm_nt(a, b):
    return lax.dot_general(a, b, (((1,), (1,)), ((), ())), preferred_element_type=F32)


def flip(size):
    r, c = iotas(size, size)
    return one_hot(r + c == size - 1)


def pack_kernel(tally_ref, ens_ref, state_ref, packed_ref, second_ref):
    pairs = 16
    patches = 2 * pairs
    rows = 8 * pairs
    half = ens_ref.shape[2] // 2
    parts = half // 256
    groups = packed_ref.shape[0] // rows
    r, k = iotas(2 * rows, 2 * rows)
    local = r & (rows - 1)
    last = r // rows
    top = (((local >> 2) & 1) ^ last) * rows
    take = one_hot(k == top + (local & 3) * patches + 2 * (local >> 3) + last)
    r2, k2 = iotas(rows, rows)
    take_s = one_hot(k2 == (r2 & 3) * patches + (r2 >> 2))
    turn = flip(256)
    r1, l1 = iotas(rows, tally_ref.shape[1])
    tally = tally_ref[...].astype(F32)
    lower = jnp.where((r1[:, :1] >> 2) & 1 == 1, float(half), 0.0)
    _, lane = iotas(rows, 256)
    lane = lane.astype(F32)
    for g in range(groups):
        own = slice(g * patches, (g + 1) * patches)
        there = slice(g * rows, (g + 1) * rows)
        wanted = l1 == 2 * ((pl.program_id(0) * groups + g) * pairs + (r1 >> 3))
        limit = jnp.sum(jnp.where(wanted, tally, 0.0), axis=1, keepdims=True) - lower
        first = []
        for q in range(parts):
            lanes = slice(q * 256, (q + 1) * 256)
            far = slice(half + q * 256, half + (q + 1) * 256)
            x = jnp.concatenate(
                [ens_ref[:, own, lanes].reshape(rows, 256), ens_ref[:, own, far].reshape(rows, 256)],
                axis=0,
            )
            both = mm(take, x)
            first.append(both[:rows])
            second_ref[(parts - 1 - q) * rows : (parts - q) * rows, :] = both[rows:].astype(BF16)
        turned = mm(second_ref[...], turn)
        for q in range(parts):
            packed_ref[there, q * 256 : (q + 1) * 256] = jnp.where(
                lane < limit - q * 256.0, first[q], turned[q * rows : (q + 1) * rows]
            ).astype(BF16)
        packed_ref[there, half:] = mm(
            take_s, state_ref[:, own, :].reshape(rows, state_ref.shape[2])
        ).astype(BF16)


def pack(tally, ens, state, interpret=False):
    members, patches, slots = ens.shape
    width = state.shape[2]
    steps = 2
    per = patches // steps
    rows = 4 * patches
    return pl.pallas_call(
        pack_kernel,
        grid=(steps,),
        in_specs=[
            pl.BlockSpec((1, patches), lambda i: (0, 0)),
            pl.BlockSpec((members, per, slots), lambda i: (0, i, 0)),
            pl.BlockSpec((members, per, width), lambda i: (0, i, 0)),
        ],
        out_specs=pl.BlockSpec((rows // steps, slots // 2 + width), lambda i: (i, 0)),
        out_shape=jax.ShapeDtypeStruct((rows, slots // 2 + width), BF16),
        scratch_shapes=[pltpu.VMEM((512, 256), BF16)],
        compiler_params=pltpu.CompilerParams(vmem_limit_bytes=PACK_VMEM),
        cost_estimate=pl.CostEstimate(
            flops=10**9, bytes_accessed=5 * 2**20, transcendentals=0
        ),
        interpret=interpret,
    )(tally.reshape(1, patches), ens, state)


def weights_kernel(me_ref, tally_ref, value_ref, prec_ref, out_ref):
    slots = value_ref.shape[1]
    row = 2 * (me_ref[0] % 4)
    count_a = tally_ref[2 * me_ref[0]]
    count_b = tally_ref[2 * me_ref[0] + 1]
    parts = slots // 256
    value = value_ref[...]
    prec = prec_ref[...]
    which, slot = iotas(8, slots)

    def pick(x, i):
        return jnp.sum(jnp.where(which == row + i, x, 0.0), axis=0, keepdims=True)

    value_b = pick(value, 1)
    prec_b = pick(prec, 1)
    cut = [b[:, i * 256 : (i + 1) * 256] for b in (value_b, prec_b) for i in range(parts)]
    r, c = iotas(256, 256)
    turn = jnp.where(r + c == 255, 1.0, 0.0)
    turned = jnp.dot(
        jnp.concatenate(cut, axis=0),
        turn,
        precision=lax.Precision.HIGHEST,
        preferred_element_type=F32,
    )
    back = [
        jnp.concatenate(
            [turned[j * parts + i : j * parts + i + 1] for i in reversed(range(parts))], axis=1
        )
        for j in range(2)
    ]
    slot = slot[:1]
    is_a = slot < count_a
    is_b = slot >= slots - count_b
    weight_a = jnp.where(is_a, jnp.sqrt(pick(prec, 0)), 0.0)
    weight_b = jnp.where(is_b & ~is_a, jnp.sqrt(back[1]), 0.0)
    seen = jnp.where(is_a, pick(value, 0), back[0])
    out_ref[0:1, :] = weight_a
    out_ref[1:2, :] = weight_b
    out_ref[2:3, :] = seen
    out_ref[3:4, :] = weight_a + weight_b
    out_ref[4:5, :] = jnp.where(is_a, 1.0, 0.0)
    out_ref[5:6, :] = jnp.where(is_a, 0.0, 1.0)
    out_ref[6:8, :] = jnp.zeros((2, slots), F32)


def pair_weights(me, tally, value, prec, interpret=False):
    slots = value.shape[1]
    return pl.pallas_call(
        weights_kernel,
        grid_spec=pltpu.PrefetchScalarGridSpec(
            num_scalar_prefetch=2,
            grid=(1,),
            in_specs=[pl.BlockSpec((8, slots), lambda i, me, t: (me[0] // 4, 0))] * 2,
            out_specs=pl.BlockSpec((8, slots), lambda i, me, t: (0, 0)),
        ),
        out_shape=jax.ShapeDtypeStruct((8, slots), F32),
        compiler_params=pltpu.CompilerParams(vmem_limit_bytes=16 * 1024 * 1024),
        interpret=interpret,
    )(me, tally, value, prec)


def split(x):
    hi = x.astype(BF16)
    return hi, (x - hi.astype(F32)).astype(BF16)


def mm3(a, b):
    ah, al = a
    bh, bl = b
    return mm(
        jnp.concatenate([ah, ah, al], axis=1), jnp.concatenate([bh, bl, bh], axis=0)
    )


def newton_schulz(ts, eye):
    a, b = ts
    cut_a, cut_b = split(a), split(b)
    z_a, z_b = 1.5 * eye - 0.5 * a, 1.5 * eye - 0.5 * b
    square_b = mm3(cut_b, cut_b)
    for step in range(1, NS_ITERS + 1):
        square_a = mm3(cut_a, cut_a) if step < NS_ITERS else None
        if step < NS_ITERS:
            cube_b = mm3(split(square_b), cut_b)
        if step > 1:
            z_a = 1.5 * z_a - 0.5 * mm3(split(z_a), cut_a)
        if step < NS_ITERS:
            cube_a = mm3(split(square_a), cut_a)
            b = 2.25 * b - 1.5 * square_b + 0.25 * cube_b
            cut_b = split(b)
            if step < NS_ITERS - 1:
                square_b = mm3(cut_b, cut_b)
            z_b = 1.5 * z_b - 0.5 * mm3(split(z_b), cut_b)
            a = 2.25 * a - 1.5 * square_a + 0.25 * cube_a
            cut_a = split(a)
    return [z_a, z_b]


def centring_matrix():
    r, k = iotas(528, 128)
    part = jnp.where(r < 512, r >> 8, r & 1)
    own = jnp.where(r < 512, ((r & 255) >> 2) * 8 + part * 4 + (r & 3), -1)
    share = jnp.where(
        ((k >> 2) & 1) == part, jnp.where(r < 512, -1.0 / 256.0, 1.0 / 256.0), 0.0
    )
    tiles = [jnp.where(own - 128 * j == k, 255.0 / 256.0, share) for j in range(4)]
    return jnp.concatenate(tiles, axis=1).astype(BF16)


def analysis_kernel(recv_ref, rows_ref, out_ref, s_ref, all_ref, perturb_ref):
    slots = rows_ref.shape[1]
    half = slots // 2
    means, middles = [[], []], []
    centre = centring_matrix()
    for q in range(half // 256):
        apart = mm(centre, recv_ref[:, q * 256 : (q + 1) * 256])
        for part in range(2):
            at = slice(part * half + q * 256, part * half + (q + 1) * 256)
            means[part].append(apart[512 + part : 513 + part])
            scaled = (apart[256 * part : 256 * (part + 1)] * rows_ref[3:4, at]).astype(BF16)
            all_ref[:, at] = scaled
            for p in range(2):
                keep = jnp.broadcast_to(rows_ref[4 + p : 5 + p, at], (256, 256)).astype(BF16)
                s_ref[256 * p : 256 * (p + 1), at] = scaled * keep
    apart = mm(centre, recv_ref[:, half:])
    for part in range(2):
        middles.append(apart[512 + part : 513 + part])
        perturb_ref[part] = apart[256 * part : 256 * (part + 1)].astype(BF16)
    means = means[0] + means[1]
    mean = jnp.concatenate(means, axis=1)
    weight_a, weight_b, seen = rows_ref[0:1, :], rows_ref[1:2, :], rows_ref[2:3, :]
    rest = []
    for w in (weight_a, weight_b):
        left = w * (seen - mean)
        for _ in range(3):
            top = left.astype(BF16).astype(F32)
            rest.append(top)
            left = left - top
    rest += [jnp.zeros_like(mean)] * 10
    s_ref[512:528, :] = jnp.concatenate(rest, axis=0).astype(BF16)
    both = mm_nt(s_ref[...], all_ref[...])
    r, c = iotas(256, 256)
    eye = jnp.where(r == c, 1.0, 0.0)
    amat = [both[256 * p : 256 * (p + 1)] + 255.0 * eye for p in range(2)]
    fro = [jnp.sqrt(jnp.sum(a * a)) for a in amat]
    z = newton_schulz([a * (1.0 / f) for a, f in zip(amat, fro)], eye)
    done = []
    for p in range(2):
        v = jnp.sum(both[512 + 3 * p : 515 + 3 * p], axis=0, keepdims=True)
        inner = jnp.sum(z[p] * v, axis=1, keepdims=True)
        mean_weights = jnp.sum(z[p] * inner, axis=0, keepdims=True) / fro[p]
        transform = (jnp.sqrt(255.0 / fro[p]) * z[p] + mean_weights).astype(BF16)
        done.append((middles[p] + mm(transform, perturb_ref[p])).astype(BF16))
    k, r = iotas(256, 256)
    scatter = one_hot(k == ((r & 127) >> 2) * 8 + (r >> 7) * 4 + (r & 3))
    for g in range(2):
        pair = jnp.concatenate([d[128 * g : 128 * (g + 1)] for d in done], axis=0)
        out_ref[256 * g : 256 * (g + 1), :] = mm(scatter, pair).astype(BF16)


def analyse(recv, rows, interpret=False):
    total, wide = recv.shape
    slots = rows.shape[1]
    width = wide - slots // 2
    return pl.pallas_call(
        analysis_kernel,
        out_shape=jax.ShapeDtypeStruct((total, width), BF16),
        scratch_shapes=[
            pltpu.VMEM((528, slots), BF16),
            pltpu.VMEM((256, slots), BF16),
            pltpu.VMEM((2, 256, width), BF16),
        ],
        compiler_params=pltpu.CompilerParams(vmem_limit_bytes=ANALYSE_VMEM),
        cost_estimate=pl.CostEstimate(
            flops=5 * 10**9, bytes_accessed=2 * 2**20, transcendentals=0
        ),
        interpret=interpret,
    )(recv, rows)


def unpack_kernel(recv_ref, out_ref):
    r, k = iotas(256, 256)
    gather = one_hot(k == (r & 63) * 4 + (r >> 6))
    for g in range(2):
        moved = mm(gather, recv_ref[256 * g : 256 * (g + 1), :]).astype(BF16)
        out_ref[:, 64 * g : 64 * (g + 1), :] = moved.reshape(4, 64, recv_ref.shape[1])


def unpack(recv, interpret=False):
    rows, width = recv.shape
    return pl.pallas_call(
        unpack_kernel,
        out_shape=jax.ShapeDtypeStruct((4, rows // 4, width), BF16),
        compiler_params=pltpu.CompilerParams(vmem_limit_bytes=16 * 1024 * 1024),
        interpret=interpret,
    )(recv)


def exchange(x):
    return lax.all_to_all(x, "mem", split_axis=0, concat_axis=0, tiled=True)


def on_device(
    background_trials, mapped_readings, measured_data, inverse_error_variance, measured_row_tally
):
    me = lax.axis_index("mem").astype(jnp.int32).reshape(1)
    packed = pack(measured_row_tally, mapped_readings, background_trials)
    received = exchange(packed)
    rows = pair_weights(me, measured_row_tally, measured_data, inverse_error_variance)
    return unpack(exchange(analyse(received, rows)))


def solution(mesh):
    return jax.shard_map(
        on_device,
        mesh=mesh,
        in_specs=(
            P("mem", "bal", None),
            P("mem", "bal", None),
            P("bal", None),
            P("bal", None),
            P("bal"),
        ),
        out_specs=P("mem", "bal", None),
        check_vma=False,
    )
```

```python
import functools

import jax
import jax.numpy as jnp
from jax import lax
from jax.experimental import pallas as pl
from jax.experimental.pallas import tpu as pltpu
from jax.sharding import PartitionSpec as P

NS_ITERS = 7
F32 = jnp.float32
BF16 = jnp.bfloat16
PACK_VMEM = 56 * 1024 * 1024
ANALYSE_VMEM = 20 * 1024 * 1024


def iotas(rows, columns):
    return (
        lax.broadcasted_iota(jnp.int32, (rows, columns), 0),
        lax.broadcasted_iota(jnp.int32, (rows, columns), 1),
    )


def one_hot(test):
    return jnp.where(test, 1.0, 0.0).astype(BF16)


def mm(a, b):
    return jnp.dot(a, b, preferred_element_type=F32)


def mm_nt(a, b):
    return lax.dot_general(a, b, (((1,), (1,)), ((), ())), preferred_element_type=F32)


def flip(size):
    r, c = iotas(size, size)
    return one_hot(r + c == size - 1)


def pack_kernel(tally_ref, ens_ref, state_ref, packed_ref, second_ref):
    pairs = 16
    patches = 2 * pairs
    rows = 8 * pairs
    half = ens_ref.shape[2] // 2
    parts = half // 256
    groups = packed_ref.shape[0] // rows
    r, k = iotas(2 * rows, 2 * rows)
    local = r & (rows - 1)
    last = r // rows
    top = (((local >> 2) & 1) ^ last) * rows
    take = one_hot(k == top + (local & 3) * patches + 2 * (local >> 3) + last)
    r2, k2 = iotas(rows, rows)
    take_s = one_hot(k2 == (r2 & 3) * patches + (r2 >> 2))
    turn = flip(256)
    r1, l1 = iotas(rows, tally_ref.shape[1])
    tally = tally_ref[...].astype(F32)
    lower = jnp.where((r1[:, :1] >> 2) & 1 == 1, float(half), 0.0)
    _, lane = iotas(rows, 256)
    lane = lane.astype(F32)
    for g in range(groups):
        own = slice(g * patches, (g + 1) * patches)
        there = slice(g * rows, (g + 1) * rows)
        wanted = l1 == 2 * ((pl.program_id(0) * groups + g) * pairs + (r1 >> 3))
        limit = jnp.sum(jnp.where(wanted, tally, 0.0), axis=1, keepdims=True) - lower
        first = []
        for q in range(parts):
            lanes = slice(q * 256, (q + 1) * 256)
            far = slice(half + q * 256, half + (q + 1) * 256)
            x = jnp.concatenate(
                [ens_ref[:, own, lanes].reshape(rows, 256), ens_ref[:, own, far].reshape(rows, 256)],
                axis=0,
            )
            both = mm(take, x)
            first.append(both[:rows])
            second_ref[(parts - 1 - q) * rows : (parts - q) * rows, :] = both[rows:].astype(BF16)
        turned = mm(second_ref[...], turn)
        for q in range(parts):
            packed_ref[there, q * 256 : (q + 1) * 256] = jnp.where(
                lane < limit - q * 256.0, first[q], turned[q * rows : (q + 1) * rows]
            ).astype(BF16)
        packed_ref[there, half:] = mm(
            take_s, state_ref[:, own, :].reshape(rows, state_ref.shape[2])
        ).astype(BF16)


def pack(tally, ens, state, interpret=False):
    members, patches, slots = ens.shape
    width = state.shape[2]
    steps = 2
    per = patches // steps
    rows = 4 * patches
    return pl.pallas_call(
        pack_kernel,
        grid=(steps,),
        in_specs=[
            pl.BlockSpec((1, patches), lambda i: (0, 0)),
            pl.BlockSpec((members, per, slots), lambda i: (0, i, 0)),
            pl.BlockSpec((members, per, width), lambda i: (0, i, 0)),
        ],
        out_specs=pl.BlockSpec((rows // steps, slots // 2 + width), lambda i: (i, 0)),
        out_shape=jax.ShapeDtypeStruct((rows, slots // 2 + width), BF16),
        scratch_shapes=[pltpu.VMEM((512, 256), BF16)],
        compiler_params=pltpu.CompilerParams(vmem_limit_bytes=PACK_VMEM),
        cost_estimate=pl.CostEstimate(
            flops=10**9, bytes_accessed=5 * 2**20, transcendentals=0
        ),
        interpret=interpret,
    )(tally.reshape(1, patches), ens, state)


def weights_kernel(me_ref, tally_ref, value_ref, prec_ref, out_ref):
    slots = value_ref.shape[1]
    row = 2 * (me_ref[0] % 4)
    count_a = tally_ref[2 * me_ref[0]]
    count_b = tally_ref[2 * me_ref[0] + 1]
    parts = slots // 256
    value = value_ref[...]
    prec = prec_ref[...]
    which, slot = iotas(8, slots)

    def pick(x, i):
        return jnp.sum(jnp.where(which == row + i, x, 0.0), axis=0, keepdims=True)

    value_b = pick(value, 1)
    prec_b = pick(prec, 1)
    cut = [b[:, i * 256 : (i + 1) * 256] for b in (value_b, prec_b) for i in range(parts)]
    r, c = iotas(256, 256)
    turn = jnp.where(r + c == 255, 1.0, 0.0)
    turned = jnp.dot(
        jnp.concatenate(cut, axis=0),
        turn,
        precision=lax.Precision.HIGHEST,
        preferred_element_type=F32,
    )
    back = [
        jnp.concatenate(
            [turned[j * parts + i : j * parts + i + 1] for i in reversed(range(parts))], axis=1
        )
        for j in range(2)
    ]
    slot = slot[:1]
    is_a = slot < count_a
    is_b = slot >= slots - count_b
    weight_a = jnp.where(is_a, jnp.sqrt(pick(prec, 0)), 0.0)
    weight_b = jnp.where(is_b & ~is_a, jnp.sqrt(back[1]), 0.0)
    seen = jnp.where(is_a, pick(value, 0), back[0])
    out_ref[0:1, :] = weight_a
    out_ref[1:2, :] = weight_b
    out_ref[2:3, :] = seen
    out_ref[3:4, :] = weight_a + weight_b
    out_ref[4:5, :] = jnp.where(is_a, 1.0, 0.0)
    out_ref[5:6, :] = jnp.where(is_a, 0.0, 1.0)
    out_ref[6:8, :] = jnp.zeros((2, slots), F32)


def pair_weights(me, tally, value, prec, interpret=False):
    slots = value.shape[1]
    return pl.pallas_call(
        weights_kernel,
        grid_spec=pltpu.PrefetchScalarGridSpec(
            num_scalar_prefetch=2,
            grid=(1,),
            in_specs=[pl.BlockSpec((8, slots), lambda i, me, t: (me[0] // 4, 0))] * 2,
            out_specs=pl.BlockSpec((8, slots), lambda i, me, t: (0, 0)),
        ),
        out_shape=jax.ShapeDtypeStruct((8, slots), F32),
        compiler_params=pltpu.CompilerParams(vmem_limit_bytes=16 * 1024 * 1024),
        interpret=interpret,
    )(me, tally, value, prec)


def split(x):
    hi = x.astype(BF16)
    return hi, (x - hi.astype(F32)).astype(BF16)


def mm3(a, b):
    ah, al = a
    bh, bl = b
    return mm(
        jnp.concatenate([ah, ah, al], axis=1), jnp.concatenate([bh, bl, bh], axis=0)
    )


def newton_schulz(ts, eye):
    a, b = ts
    cut_a, cut_b = split(a), split(b)
    z_a, z_b = 1.5 * eye - 0.5 * a, 1.5 * eye - 0.5 * b
    square_b = mm3(cut_b, cut_b)
    for step in range(1, NS_ITERS + 1):
        square_a = mm3(cut_a, cut_a) if step < NS_ITERS else None
        if step < NS_ITERS:
            cube_b = mm3(split(square_b), cut_b)
        if step > 1:
            z_a = 1.5 * z_a - 0.5 * mm3(split(z_a), cut_a)
        if step < NS_ITERS:
            cube_a = mm3(split(square_a), cut_a)
            b = 2.25 * b - 1.5 * square_b + 0.25 * cube_b
            cut_b = split(b)
            if step < NS_ITERS - 1:
                square_b = mm3(cut_b, cut_b)
            z_b = 1.5 * z_b - 0.5 * mm3(split(z_b), cut_b)
            a = 2.25 * a - 1.5 * square_a + 0.25 * cube_a
            cut_a = split(a)
    return [z_a, z_b]


def centring_matrix():
    r, k = iotas(528, 128)
    part = jnp.where(r < 512, r >> 8, r & 1)
    own = jnp.where(r < 512, ((r & 255) >> 2) * 8 + part * 4 + (r & 3), -1)
    share = jnp.where(
        ((k >> 2) & 1) == part, jnp.where(r < 512, -1.0 / 256.0, 1.0 / 256.0), 0.0
    )
    tiles = [jnp.where(own - 128 * j == k, 255.0 / 256.0, share) for j in range(4)]
    return jnp.concatenate(tiles, axis=1).astype(BF16)


def analysis_kernel(recv_ref, rows_ref, out_ref, s_ref, all_ref, perturb_ref):
    slots = rows_ref.shape[1]
    half = slots // 2
    middles = []
    centre = centring_matrix()
    both = None
    for q in range(half // 256):
        apart = mm(centre, recv_ref[:, q * 256 : (q + 1) * 256])
        for part in range(2):
            at = slice(part * half + q * 256, part * half + (q + 1) * 256)
            mean = apart[512 + part : 513 + part]
            scaled = (apart[256 * part : 256 * (part + 1)] * rows_ref[3:4, at]).astype(BF16)
            all_ref[:, at] = scaled
            for p in range(2):
                keep = jnp.broadcast_to(rows_ref[4 + p : 5 + p, at], (256, 256)).astype(BF16)
                s_ref[256 * p : 256 * (p + 1), at] = scaled * keep
            rest = []
            for p in range(2):
                left = rows_ref[p : p + 1, at] * (rows_ref[2:3, at] - mean)
                for _ in range(3):
                    top = left.astype(BF16).astype(F32)
                    rest.append(top)
                    left = left - top
            rest.append(jnp.zeros((10, 256), F32))
            s_ref[512:528, at] = jnp.concatenate(rest, axis=0).astype(BF16)
        if q % 2 == 2 - 1:
            for part in range(2):
                at = slice(part * half + (q + 1 - 2) * 256, part * half + (q + 1) * 256)
                more = mm_nt(s_ref[:, at], all_ref[:, at])
                both = more if both is None else both + more
    apart = mm(centre, recv_ref[:, half:])
    for part in range(2):
        middles.append(apart[512 + part : 513 + part])
        perturb_ref[part] = apart[256 * part : 256 * (part + 1)].astype(BF16)
    r, c = iotas(256, 256)
    eye = jnp.where(r == c, 1.0, 0.0)
    amat = [both[256 * p : 256 * (p + 1)] + 255.0 * eye for p in range(2)]
    fro = [
        jnp.sqrt(jnp.sum(jnp.sum(a * a, axis=0, keepdims=True), axis=1, keepdims=True))
        for a in amat
    ]
    z = newton_schulz([a * (1.0 / f) for a, f in zip(amat, fro)], eye)
    done = []
    for p in (1, 0):
        v = jnp.sum(both[512 + 3 * p : 515 + 3 * p], axis=0, keepdims=True)
        inner = jnp.sum(z[p] * v, axis=1, keepdims=True)
        mean_weights = jnp.sum(z[p] * inner, axis=0, keepdims=True) / fro[p]
        transform = (jnp.sqrt(255.0 / fro[p]) * z[p] + mean_weights).astype(BF16)
        done.append((middles[p] + mm(transform, perturb_ref[p])).astype(BF16))
    k, r = iotas(256, 256)
    scatter = one_hot(k == ((r & 127) >> 2) * 8 + (r >> 7) * 4 + (r & 3))
    for g in range(2):
        pair = jnp.concatenate([d[128 * g : 128 * (g + 1)] for d in done[::-1]], axis=0)
        out_ref[256 * g : 256 * (g + 1), :] = mm(scatter, pair).astype(BF16)


def analyse(recv, rows, interpret=False):
    total, wide = recv.shape
    slots = rows.shape[1]
    width = wide - slots // 2
    return pl.pallas_call(
        analysis_kernel,
        out_shape=jax.ShapeDtypeStruct((total, width), BF16),
        scratch_shapes=[
            pltpu.VMEM((528, slots), BF16),
            pltpu.VMEM((256, slots), BF16),
            pltpu.VMEM((2, 256, width), BF16),
        ],
        compiler_params=pltpu.CompilerParams(vmem_limit_bytes=ANALYSE_VMEM),
        cost_estimate=pl.CostEstimate(
            flops=5 * 10**9, bytes_accessed=2 * 2**20, transcendentals=0
        ),
        interpret=interpret,
    )(recv, rows)


def unpack_kernel(recv_ref, out_ref):
    r, k = iotas(256, 256)
    gather = one_hot(k == (r & 63) * 4 + (r >> 6))
    for g in range(2):
        moved = mm(gather, recv_ref[256 * g : 256 * (g + 1), :]).astype(BF16)
        out_ref[:, 64 * g : 64 * (g + 1), :] = moved.reshape(4, 64, recv_ref.shape[1])


def unpack(recv, interpret=False):
    rows, width = recv.shape
    return pl.pallas_call(
        unpack_kernel,
        out_shape=jax.ShapeDtypeStruct((4, rows // 4, width), BF16),
        compiler_params=pltpu.CompilerParams(vmem_limit_bytes=16 * 1024 * 1024),
        interpret=interpret,
    )(recv)


def exchange(x):
    return lax.all_to_all(x, "mem", split_axis=0, concat_axis=0, tiled=True)


def on_device(
    background_trials, mapped_readings, measured_data, inverse_error_variance, measured_row_tally
):
    me = lax.axis_index("mem").astype(jnp.int32).reshape(1)
    packed = pack(measured_row_tally, mapped_readings, background_trials)
    received = exchange(packed)
    rows = pair_weights(me, measured_row_tally, measured_data, inverse_error_variance)
    return unpack(exchange(analyse(received, rows)))


def solution(mesh):
    return jax.shard_map(
        on_device,
        mesh=mesh,
        in_specs=(
            P("mem", "bal", None),
            P("mem", "bal", None),
            P("bal", None),
            P("bal", None),
            P("bal"),
        ),
        out_specs=P("mem", "bal", None),
        check_vma=False,
    )
```

```python
import functools

import jax
import jax.numpy as jnp
from jax import lax
from jax.experimental import pallas as pl
from jax.experimental.pallas import tpu as pltpu
from jax.sharding import PartitionSpec as P

NS_ITERS = 7
F32 = jnp.float32
BF16 = jnp.bfloat16
PACK_VMEM = 56 * 1024 * 1024
ANALYSE_VMEM = 20 * 1024 * 1024


def iotas(rows, columns):
    return (
        lax.broadcasted_iota(jnp.int32, (rows, columns), 0),
        lax.broadcasted_iota(jnp.int32, (rows, columns), 1),
    )


def one_hot(test):
    return jnp.where(test, 1.0, 0.0).astype(BF16)


def mm(a, b):
    return jnp.dot(a, b, preferred_element_type=F32)


def mm_nt(a, b):
    return lax.dot_general(a, b, (((1,), (1,)), ((), ())), preferred_element_type=F32)


def flip(size):
    r, c = iotas(size, size)
    return one_hot(r + c == size - 1)


def pack_kernel(tally_ref, ens_ref, state_ref, packed_ref, second_ref):
    pairs = 16
    patches = 2 * pairs
    rows = 8 * pairs
    half = ens_ref.shape[2] // 2
    parts = half // 256
    groups = packed_ref.shape[0] // rows
    r, k = iotas(2 * rows, 2 * rows)
    local = r & (rows - 1)
    last = r // rows
    top = (((local >> 2) & 1) ^ last) * rows
    take = one_hot(k == top + (local & 3) * patches + 2 * (local >> 3) + last)
    r2, k2 = iotas(rows, rows)
    take_s = one_hot(k2 == (r2 & 3) * patches + (r2 >> 2))
    turn = flip(256)
    r1, l1 = iotas(rows, tally_ref.shape[1])
    tally = tally_ref[...].astype(F32)
    lower = jnp.where((r1[:, :1] >> 2) & 1 == 1, float(half), 0.0)
    _, lane = iotas(rows, 256)
    lane = lane.astype(F32)
    firsts = []
    for g in range(groups):
        own = slice(g * patches, (g + 1) * patches)
        for q in range(parts):
            lanes = slice(q * 256, (q + 1) * 256)
            far = slice(half + q * 256, half + (q + 1) * 256)
            x = jnp.concatenate(
                [ens_ref[:, own, lanes].reshape(rows, 256), ens_ref[:, own, far].reshape(rows, 256)],
                axis=0,
            )
            both = mm(take, x)
            firsts.append(both[:rows])
            second_ref[g, (parts - 1 - q) * rows : (parts - q) * rows, :] = both[rows:].astype(BF16)
    for g in range(groups):
        own = slice(g * patches, (g + 1) * patches)
        there = slice(g * rows, (g + 1) * rows)
        packed_ref[there, half:] = mm(
            take_s, state_ref[:, own, :].reshape(rows, state_ref.shape[2])
        ).astype(BF16)
        wanted = l1 == 2 * ((pl.program_id(0) * groups + g) * pairs + (r1 >> 3))
        limit = jnp.sum(jnp.where(wanted, tally, 0.0), axis=1, keepdims=True) - lower
        turned = mm(second_ref[g], turn)
        for q in range(parts):
            packed_ref[there, q * 256 : (q + 1) * 256] = jnp.where(
                lane < limit - q * 256.0, firsts[g * parts + q], turned[q * rows : (q + 1) * rows]
            ).astype(BF16)


def pack(tally, ens, state, interpret=False):
    members, patches, slots = ens.shape
    width = state.shape[2]
    steps = 2
    per = patches // steps
    rows = 4 * patches
    return pl.pallas_call(
        pack_kernel,
        grid=(steps,),
        in_specs=[
            pl.BlockSpec((1, patches), lambda i: (0, 0)),
            pl.BlockSpec((members, per, slots), lambda i: (0, i, 0)),
            pl.BlockSpec((members, per, width), lambda i: (0, i, 0)),
        ],
        out_specs=pl.BlockSpec((rows // steps, slots // 2 + width), lambda i: (i, 0)),
        out_shape=jax.ShapeDtypeStruct((rows, slots // 2 + width), BF16),
        scratch_shapes=[pltpu.VMEM((2, 512, 256), BF16)],
        compiler_params=pltpu.CompilerParams(vmem_limit_bytes=PACK_VMEM),
        cost_estimate=pl.CostEstimate(
            flops=10**9, bytes_accessed=5 * 2**20, transcendentals=0
        ),
        interpret=interpret,
    )(tally.reshape(1, patches), ens, state)


def weights_kernel(me_ref, tally_ref, value_ref, prec_ref, out_ref):
    slots = value_ref.shape[1]
    row = 2 * (me_ref[0] % 4)
    count_a = tally_ref[2 * me_ref[0]]
    count_b = tally_ref[2 * me_ref[0] + 1]
    parts = slots // 256
    value = value_ref[...]
    prec = prec_ref[...]
    which, slot = iotas(8, slots)

    def pick(x, i):
        return jnp.sum(jnp.where(which == row + i, x, 0.0), axis=0, keepdims=True)

    value_b = pick(value, 1)
    prec_b = pick(prec, 1)
    cut = [b[:, i * 256 : (i + 1) * 256] for b in (value_b, prec_b) for i in range(parts)]
    r, c = iotas(256, 256)
    turn = jnp.where(r + c == 255, 1.0, 0.0)
    turned = jnp.dot(
        jnp.concatenate(cut, axis=0),
        turn,
        precision=lax.Precision.HIGHEST,
        preferred_element_type=F32,
    )
    back = [
        jnp.concatenate(
            [turned[j * parts + i : j * parts + i + 1] for i in reversed(range(parts))], axis=1
        )
        for j in range(2)
    ]
    slot = slot[:1]
    is_a = slot < count_a
    is_b = slot >= slots - count_b
    weight_a = jnp.where(is_a, jnp.sqrt(pick(prec, 0)), 0.0)
    weight_b = jnp.where(is_b & ~is_a, jnp.sqrt(back[1]), 0.0)
    seen = jnp.where(is_a, pick(value, 0), back[0])
    out_ref[0:1, :] = weight_a
    out_ref[1:2, :] = weight_b
    out_ref[2:3, :] = seen
    out_ref[3:4, :] = weight_a + weight_b
    out_ref[4:5, :] = jnp.where(is_a, 1.0, 0.0)
    out_ref[5:6, :] = jnp.where(is_a, 0.0, 1.0)
    out_ref[6:8, :] = jnp.zeros((2, slots), F32)


def pair_weights(me, tally, value, prec, interpret=False):
    slots = value.shape[1]
    return pl.pallas_call(
        weights_kernel,
        grid_spec=pltpu.PrefetchScalarGridSpec(
            num_scalar_prefetch=2,
            grid=(1,),
            in_specs=[pl.BlockSpec((8, slots), lambda i, me, t: (me[0] // 4, 0))] * 2,
            out_specs=pl.BlockSpec((8, slots), lambda i, me, t: (0, 0)),
        ),
        out_shape=jax.ShapeDtypeStruct((8, slots), F32),
        compiler_params=pltpu.CompilerParams(vmem_limit_bytes=16 * 1024 * 1024),
        interpret=interpret,
    )(me, tally, value, prec)


def split(x):
    hi = x.astype(BF16)
    return hi, (x - hi.astype(F32)).astype(BF16)


def mm3(a, b):
    ah, al = a
    bh, bl = b
    return mm(
        jnp.concatenate([ah, ah, al], axis=1), jnp.concatenate([bh, bl, bh], axis=0)
    )


def newton_schulz(ts, eye):
    a, b = ts
    cut_a, cut_b = split(a), split(b)
    z_a, z_b = 1.5 * eye - 0.5 * a, 1.5 * eye - 0.5 * b
    square_b = mm3(cut_b, cut_b)
    for step in range(1, NS_ITERS + 1):
        square_a = mm3(cut_a, cut_a) if step < NS_ITERS else None
        if step < NS_ITERS:
            cube_b = mm3(split(square_b), cut_b)
        if step > 1:
            z_a = 1.5 * z_a - 0.5 * mm3(split(z_a), cut_a)
        if step < NS_ITERS:
            cube_a = mm3(split(square_a), cut_a)
            b = 2.25 * b - 1.5 * square_b + 0.25 * cube_b
            cut_b = split(b)
            if step < NS_ITERS - 1:
                square_b = mm3(cut_b, cut_b)
            z_b = 1.5 * z_b - 0.5 * mm3(split(z_b), cut_b)
            a = 2.25 * a - 1.5 * square_a + 0.25 * cube_a
            cut_a = split(a)
    return [z_a, z_b]


def centring_matrix():
    r, k = iotas(528, 128)
    part = jnp.where(r < 512, r >> 8, r & 1)
    own = jnp.where(r < 512, ((r & 255) >> 2) * 8 + part * 4 + (r & 3), -1)
    share = jnp.where(
        ((k >> 2) & 1) == part, jnp.where(r < 512, -1.0 / 256.0, 1.0 / 256.0), 0.0
    )
    tiles = [jnp.where(own - 128 * j == k, 255.0 / 256.0, share) for j in range(4)]
    return jnp.concatenate(tiles, axis=1).astype(BF16)


def analysis_kernel(recv_ref, rows_ref, out_ref, s_ref, all_ref, perturb_ref):
    slots = rows_ref.shape[1]
    half = slots // 2
    middles = []
    centre = centring_matrix()
    both = None
    for q in range(half // 256):
        apart = mm(centre, recv_ref[:, q * 256 : (q + 1) * 256])
        for part in range(2):
            at = slice(part * half + q * 256, part * half + (q + 1) * 256)
            mean = apart[512 + part : 513 + part]
            scaled = (apart[256 * part : 256 * (part + 1)] * rows_ref[3:4, at]).astype(BF16)
            all_ref[:, at] = scaled
            for p in range(2):
                keep = jnp.broadcast_to(rows_ref[4 + p : 5 + p, at], (256, 256)).astype(BF16)
                s_ref[256 * p : 256 * (p + 1), at] = scaled * keep
            rest = []
            for p in range(2):
                left = rows_ref[p : p + 1, at] * (rows_ref[2:3, at] - mean)
                for _ in range(3):
                    top = left.astype(BF16).astype(F32)
                    rest.append(top)
                    left = left - top
            rest.append(jnp.zeros((10, 256), F32))
            s_ref[512:528, at] = jnp.concatenate(rest, axis=0).astype(BF16)
        if q % 2 == 2 - 1:
            for part in range(2):
                at = slice(part * half + (q + 1 - 2) * 256, part * half + (q + 1) * 256)
                more = mm_nt(s_ref[:, at], all_ref[:, at])
                both = more if both is None else both + more
    apart = mm(centre, recv_ref[:, half:])
    for part in range(2):
        middles.append(apart[512 + part : 513 + part])
        perturb_ref[part] = apart[256 * part : 256 * (part + 1)].astype(BF16)
    r, c = iotas(256, 256)
    eye = jnp.where(r == c, 1.0, 0.0)
    amat = [both[256 * p : 256 * (p + 1)] + 255.0 * eye for p in range(2)]
    fro = [
        jnp.sqrt(jnp.sum(jnp.sum(a * a, axis=0, keepdims=True), axis=1, keepdims=True))
        for a in amat
    ]
    z = newton_schulz([a * (1.0 / f) for a, f in zip(amat, fro)], eye)
    done = []
    for p in (1, 0):
        v = jnp.sum(both[512 + 3 * p : 515 + 3 * p], axis=0, keepdims=True)
        inner = jnp.sum(z[p] * v, axis=1, keepdims=True)
        mean_weights = jnp.sum(z[p] * inner, axis=0, keepdims=True) / fro[p]
        transform = (jnp.sqrt(255.0 / fro[p]) * z[p] + mean_weights).astype(BF16)
        done.append((middles[p] + mm(transform, perturb_ref[p])).astype(BF16))
    k, r = iotas(256, 256)
    scatter = one_hot(k == ((r & 127) >> 2) * 8 + (r >> 7) * 4 + (r & 3))
    for g in range(2):
        pair = jnp.concatenate([d[128 * g : 128 * (g + 1)] for d in done[::-1]], axis=0)
        out_ref[256 * g : 256 * (g + 1), :] = mm(scatter, pair).astype(BF16)


def analyse(recv, rows, interpret=False):
    total, wide = recv.shape
    slots = rows.shape[1]
    width = wide - slots // 2
    return pl.pallas_call(
        analysis_kernel,
        out_shape=jax.ShapeDtypeStruct((total, width), BF16),
        scratch_shapes=[
            pltpu.VMEM((528, slots), BF16),
            pltpu.VMEM((256, slots), BF16),
            pltpu.VMEM((2, 256, width), BF16),
        ],
        compiler_params=pltpu.CompilerParams(vmem_limit_bytes=ANALYSE_VMEM),
        cost_estimate=pl.CostEstimate(
            flops=5 * 10**9, bytes_accessed=2 * 2**20, transcendentals=0
        ),
        interpret=interpret,
    )(recv, rows)


def unpack_kernel(recv_ref, out_ref):
    r, k = iotas(256, 256)
    gather = one_hot(k == (r & 63) * 4 + (r >> 6))
    for g in range(2):
        moved = mm(gather, recv_ref[256 * g : 256 * (g + 1), :]).astype(BF16)
        out_ref[:, 64 * g : 64 * (g + 1), :] = moved.reshape(4, 64, recv_ref.shape[1])


def unpack(recv, interpret=False):
    rows, width = recv.shape
    return pl.pallas_call(
        unpack_kernel,
        out_shape=jax.ShapeDtypeStruct((4, rows // 4, width), BF16),
        compiler_params=pltpu.CompilerParams(vmem_limit_bytes=16 * 1024 * 1024),
        interpret=interpret,
    )(recv)


def exchange(x):
    return lax.all_to_all(x, "mem", split_axis=0, concat_axis=0, tiled=True)


def on_device(
    background_trials, mapped_readings, measured_data, inverse_error_variance, measured_row_tally
):
    me = lax.axis_index("mem").astype(jnp.int32).reshape(1)
    packed = pack(measured_row_tally, mapped_readings, background_trials)
    received = exchange(packed)
    rows = pair_weights(me, measured_row_tally, measured_data, inverse_error_variance)
    return unpack(exchange(analyse(received, rows)))


def solution(mesh):
    return jax.shard_map(
        on_device,
        mesh=mesh,
        in_specs=(
            P("mem", "bal", None),
            P("mem", "bal", None),
            P("bal", None),
            P("bal", None),
            P("bal"),
        ),
        out_specs=P("mem", "bal", None),
        check_vma=False,
    )
```
